32 devices in a mesh: ex: 4 (over z), ctx: 8 (over y, x, core).
Axes of the slice: x: 2, y: 2, z: 4, core: 2. Of those that a mesh axis runs over, the one named last changes fastest.
Arguments:
- stream: bfloat16 [4, 256, 8192], P('ex', None, 'ctx'), may hold values from -6 to 6
- cotangent: bfloat16 [4, 256, 8192], P('ex', None, 'ctx'), may hold values from -6 to 6
- base_ids: int32 [4, 8192], P('ex', 'ctx'), may hold values from 0 to 4
- clip_bound: int32 [4], P('ex'), may hold values from 1 to 4
- w_value: bfloat16 [256, 256], replicated, may hold values from -2 to 2
- w_gate: bfloat16 [256, 256], replicated, may hold values from -0.375 to 0.375
- filter_taps: float32 [256, 8192], P('ctx', 'ex'), may hold values from -0.0625 to 0.0625
- filter_bias: float32 [256], P('ctx'), may hold values from 0.1 to 1.9
Outputs:
- input_grad: bfloat16 [4, 256, 8192], P('ex', None, 'ctx')
- filter_grad: float32 [256, 8192], P('ctx', 'ex')
The draws below stay inside these ranges and needn't reach their ends.
All inputs are finite; a program needn't handle non-finite values.
Results may differ from the reference program's by a relative error of at most 0.015.
Values may be sent and summed in bfloat16 or wider, within the bound.
A program may use at most 128 MiB of HBM per device.

```python
import jax
import jax.numpy as jnp
from jax import lax

D = 256
TOK_DEV = 1024
LENGTH = 8192
EXAMPLES = 4
N_CTX = 8


def draw_w_value(key, part):
    key_entries = jax.random.fold_in(key, 11)
    key_jitter = jax.random.fold_in(key, 12)
    rising = 0.3 * 10.0 ** (jnp.arange(D, dtype=jnp.float32) / D)
    jitter = jnp.exp(jax.random.uniform(key_jitter, (D,), jnp.float32, -0.35, 0.35))
    row_scale = rising * jitter
    entries = jax.random.normal(key_entries, (D, D), jnp.float32)
    return (row_scale[:, None] * entries / jnp.sqrt(jnp.float32(D))).astype(jnp.bfloat16)


def with_ends(values, own_key, low, high):
    index_at = [jax.random.randint(jax.random.fold_in(own_key, axis), (), 0, length) for axis, length in enumerate(values.shape)]
    longest = values.shape.index(max(values.shape))
    next_to = index_at[:longest] + [(index_at[longest] + 1) % values.shape[longest]] + index_at[longest + 1:]
    return values.at[tuple(index_at)].set(low).at[tuple(next_to)].set(high)


def block_scale(key, dims, shards, low, high):
    level, own = 1.0, jax.random.fold_in(key, 6)
    for dim, blocks in shards:
        draws = jnp.exp(jax.random.uniform(jax.random.fold_in(own, dim), (blocks,), jnp.float32, low / len(shards), high / len(shards)))
        level = level * jnp.repeat(draws, dims[dim] // blocks).reshape([-1 if axis == dim else 1 for axis in range(len(dims))])
    return level


def noise(stream_key, shape, scale, most, cuts=(), held_as=jnp.bfloat16):
    factor_of = block_scale(stream_key, shape, cuts, -0.22, 0.18) if cuts else 1.0
    values = jax.random.normal(stream_key, shape, jnp.float32) * scale * factor_of
    return jnp.minimum(jnp.maximum(values, -most), most).astype(held_as)


def setup_inputs(seed: int = 0) -> dict:
    seeds = jax.random.split(jax.random.key(seed), 9)
    stream = noise(seeds[0], (EXAMPLES, D, LENGTH), 1.0, 6.0, ((0, 4), (2, 8)))
    cotangent = noise(seeds[1], (EXAMPLES, D, LENGTH), 1.0, 6.0, ((0, 4), (2, 8)))
    base_ids = with_ends(jax.random.randint(seeds[2], (EXAMPLES, LENGTH), 0, 5), jax.random.fold_in(seeds[2], 1), 0, 4).astype(jnp.int32)
    clip_bound = with_ends(jax.random.randint(seeds[3], (EXAMPLES,), 1, 5), jax.random.fold_in(seeds[3], 1), 1, 4).astype(jnp.int32)
    w_value = draw_w_value(jax.random.fold_in(seeds[8], 71), 0)
    w_gate = noise(seeds[5], (D, D), D ** -0.5, 0.375)
    filter_taps = noise(seeds[6], (D, LENGTH), (TOK_DEV * N_CTX) ** -0.5, 0.0625, ((0, 8), (1, 4)), jnp.float32)
    filter_bias = jnp.clip(1.0 + 0.18 * jax.random.normal(seeds[7], (D,), jnp.float32), 0.1, 1.9)
    return {"stream": stream, "cotangent": cotangent, "base_ids": base_ids, "clip_bound": clip_bound, "w_value": w_value, "w_gate": w_gate, "filter_taps": filter_taps, "filter_bias": filter_bias}


unknown_base = 4

def reference(stream, cotangent, base_ids, clip_bound, w_value, w_gate, filter_taps, filter_bias):
    seq_len = stream.shape[2]
    fft_len = 2 * seq_len
    taps_spec = jnp.fft.rfft(filter_taps, n=fft_len, axis=1)
    bias_col = filter_bias[:, None]

    def one_example(running, items):
        tokens_in, cot_raw, ids_row, bound_raw = items
        value = jnp.dot(w_value, tokens_in, preferred_element_type=jnp.float32).astype(jnp.bfloat16)
        gate = jnp.dot(w_gate, tokens_in, preferred_element_type=jnp.float32).astype(jnp.bfloat16)
        keep_mask = (ids_row != unknown_base).astype(jnp.float32)
        masked_cot = (cot_raw.astype(jnp.float32) * keep_mask[None, :]).astype(jnp.bfloat16)
        signal_grad = (gate.astype(jnp.float32) * masked_cot.astype(jnp.float32)).astype(jnp.bfloat16)
        value_wide = value.astype(jnp.float32)
        signal_wide = signal_grad.astype(jnp.float32)
        value_spec = jnp.fft.rfft(value_wide, n=fft_len, axis=1)
        signal_spec = jnp.fft.rfft(signal_wide, n=fft_len, axis=1)
        conv_out = jnp.fft.irfft(taps_spec * value_spec, n=fft_len, axis=1)[:, :seq_len]
        conv_state = (conv_out + bias_col * value_wide).astype(jnp.bfloat16)
        back_out = jnp.fft.irfft(jnp.conj(taps_spec) * signal_spec, n=fft_len, axis=1)[:, :seq_len]
        value_grad = (back_out + bias_col * signal_wide).astype(jnp.bfloat16)
        gate_grad = (conv_state.astype(jnp.float32) * masked_cot.astype(jnp.float32)).astype(jnp.bfloat16)
        input_grad = jnp.dot(w_value.T, value_grad, preferred_element_type=jnp.float32)
        input_grad = input_grad + jnp.dot(w_gate.T, gate_grad, preferred_element_type=jnp.float32)
        taps_grad = jnp.fft.irfft(signal_spec * jnp.conj(value_spec), n=fft_len, axis=1)[:, :seq_len]
        rms = jnp.sqrt(jnp.mean(taps_grad * taps_grad) + 1e-06)
        factor = jnp.minimum(1.0, bound_raw.astype(jnp.float32) / rms)
        return (running + factor * taps_grad, input_grad.astype(jnp.bfloat16))
    start_sum = jnp.zeros(filter_taps.shape, jnp.float32)
    filter_grad, input_grad = lax.scan(one_example, start_sum, (stream, cotangent, base_ids, clip_bound))
    return (input_grad, filter_grad)
```

```python
import functools
import math

import jax
import jax.numpy as jnp
import numpy as np
from jax import lax
from jax.experimental import pallas as pl
from jax.experimental.pallas import tpu as pltpu
from jax.sharding import PartitionSpec as P

LANES = 128
UNKNOWN = 4
EPS = 1e-06
F32 = jnp.float32
BF16 = jnp.bfloat16
MESH = pl.DeviceIdType.MESH


def tables(rows):
    whole = 2 * rows * LANES
    ka = np.arange(rows) + 0.5
    a = np.arange(rows)
    r = np.arange(LANES)
    outer = 2 * math.pi * ka[:, None] * a[None, :] / (2 * rows)
    inner = 2 * math.pi * (r[:, None] * r[None, :] % LANES) / LANES
    twist = 2 * math.pi * ka[:, None] * r[None, :] / whole
    cos, sin = np.cos(inner), np.sin(inner)
    first = np.concatenate([np.cos(outer), -np.sin(outer)], 0)
    last = np.concatenate([np.cos(outer).T, -np.sin(outer).T], 1)
    second = np.block([[cos, -sin], [sin, cos]])
    third = np.block([[cos, sin], [-sin, cos]])
    twist = np.stack([np.cos(twist), np.sin(twist)])
    return (
        jnp.asarray(first, BF16),
        jnp.asarray(second, BF16),
        jnp.asarray(third, BF16),
        jnp.asarray(last, BF16),
        jnp.asarray(twist, F32),
    )


def dot(x, y):
    return jnp.dot(x, y, preferred_element_type=F32)


def stack_rows(blocks):
    if blocks[0].shape[0] % 16 == 0:
        return jnp.concatenate(blocks, 0)
    return jnp.concatenate([b.astype(F32) for b in blocks], 0).astype(BF16)


def kernel(
    n_ctx, n_ex, halves, group,
    stream, cotangent, ids, bound, w_value, w_gate, taps, bias,
    first, second, third, last, twist,
    input_grad, filter_grad,
    in_send, in_recv, out_send, out_recv, tap_send, tap_recv, grad_send, grad_recv,
    sq_send, sq_recv, fac_send, fac_recv,
    val_wide, sig_wide, fil_wide, conv_wide, back_wide, tapg_wide,
    in_ss, in_rs, out_ss, out_rs, tap_ss, tap_rs, grad_ss, grad_rs,
    sq_ss, sq_rs, fac_ss, fac_rs,
):
    ex = lax.axis_index("ex")
    ctx = lax.axis_index("ctx")
    ctx_peers = [lax.rem(ctx + i, n_ctx) for i in range(1, n_ctx)]
    ex_peers = [lax.rem(ex + i, n_ex) for i in range(1, n_ex)]
    depth = stream.shape[1]
    tokens = stream.shape[2]
    chans = taps.shape[0]
    part = chans // halves
    tiles = tokens // LANES
    rows = n_ctx * tiles
    lag_tiles = rows // n_ex

    def to_ctx(src, dst, ss, rs, peer):
        return pltpu.make_async_remote_copy(
            src_ref=src, dst_ref=dst, send_sem=ss, recv_sem=rs,
            device_id=(ex, peer), device_id_type=MESH,
        )

    def to_ex(src, dst, ss, rs, peer):
        return pltpu.make_async_remote_copy(
            src_ref=src, dst_ref=dst, send_sem=ss, recv_sem=rs,
            device_id=(peer, ctx), device_id_type=MESH,
        )

    barrier = pltpu.get_barrier_semaphore()
    for peer in ctx_peers:
        pl.semaphore_signal(barrier, inc=1, device_id=(ex, peer), device_id_type=MESH)
    for peer in ex_peers:
        pl.semaphore_signal(barrier, inc=1, device_id=(peer, ctx), device_id_type=MESH)

    tap_send[...] = taps[...].astype(BF16)
    keep = ids[...] != UNKNOWN

    width = min(256, tokens)
    tok = stream[0]
    for lo in range(0, tokens, width):
        cols = slice(lo, lo + width)
        value = dot(w_value[...], tok[:, cols])
        gate = dot(w_gate[...], tok[:, cols]).astype(BF16).astype(F32)
        cot = jnp.where(keep[:, cols], cotangent[0, :, cols].astype(F32), 0.0)
        signal = gate * cot
        for d in range(n_ctx):
            for h in range(halves):
                at = d * chans + h * part
                in_send[h, d, 0, :, cols] = value[at:at + part].astype(BF16)
                in_send[h, d, 1, :, cols] = signal[at:at + part].astype(BF16)

    pl.semaphore_wait(barrier, n_ctx - 1 + n_ex - 1)
    for peer in ex_peers:
        to_ex(tap_send, tap_recv.at[ex], tap_ss.at[peer], tap_rs.at[ex], peer).start()
    for h in range(halves):
        for peer in ctx_peers:
            to_ctx(
                in_send.at[h, peer], in_recv.at[h, ctx],
                in_ss.at[h, peer], in_rs.at[h, ctx], peer,
            ).start()
    tap_recv[ex] = tap_send[...]
    for h in range(halves):
        in_recv[h, ctx] = in_send[h, ctx]
    for peer in ex_peers:
        to_ex(tap_send, tap_recv.at[peer], tap_ss.at[peer], tap_rs.at[peer], peer).wait_recv()

    g_first, g_second, g_third, g_last = first[...], second[...], third[...], last[...]
    scale = 1.0 / (rows * LANES)
    square = jnp.zeros((8, LANES), F32)

    for h in range(halves):
        chan_lo = h * part
        for e in range(n_ex):
            for j in range(lag_tiles):
                at = (e * lag_tiles + j) * part
                fil_wide[at:at + part, :] = tap_recv[
                    e, chan_lo:chan_lo + part, j * LANES:(j + 1) * LANES
                ].astype(F32)
        for peer in ctx_peers:
            to_ctx(
                in_send.at[h, peer], in_recv.at[h, peer],
                in_ss.at[h, peer], in_rs.at[h, peer], peer,
            ).wait_recv()
        for d in range(n_ctx):
            for j in range(tiles):
                at = (d * tiles + j) * part
                cols = slice(j * LANES, (j + 1) * LANES)
                val_wide[at:at + part, :] = in_recv[h, d, 0, :, cols].astype(F32)
                sig_wide[at:at + part, :] = in_recv[h, d, 1, :, cols].astype(F32)

        def some_channels(step, carry):
            base = step * group
            pick = lambda c: pl.ds(base + c, rows, stride=part)
            flat = []
            for c in range(group):
                for ref in (fil_wide, val_wide, sig_wide):
                    flat.append(ref[pick(c), :].astype(BF16))
            mid = dot(g_first, jnp.concatenate(flat, 1))
            t_cos, t_sin = twist[0], twist[1]
            blocks = []
            for m in range(3 * group):
                re = mid[:rows, m * LANES:(m + 1) * LANES]
                im = mid[rows:, m * LANES:(m + 1) * LANES]
                blocks.append(jnp.concatenate(
                    [re * t_cos + im * t_sin, im * t_cos - re * t_sin], 1
                ).astype(BF16))
            spec = dot(jnp.concatenate(blocks, 0), g_second)
            blocks = []
            for c in range(group):
                parts = []
                for m in range(3):
                    at = (3 * c + m) * rows
                    parts.append(spec[at:at + rows, :LANES])
                    parts.append(spec[at:at + rows, LANES:])
                fr, fi, vr, vi, sr, si = parts
                blocks.append(jnp.concatenate([fr * vr - fi * vi, fr * vi + fi * vr], 1).astype(BF16))
                blocks.append(jnp.concatenate([fr * sr + fi * si, fr * si - fi * sr], 1).astype(BF16))
                blocks.append(jnp.concatenate([sr * vr + si * vi, si * vr - sr * vi], 1).astype(BF16))
            back = dot(jnp.concatenate(blocks, 0), g_third)
            flat = []
            u_cos, u_sin = t_cos * scale, t_sin * scale
            for m in range(3 * group):
                re = back[m * rows:(m + 1) * rows, :LANES]
                im = back[m * rows:(m + 1) * rows, LANES:]
                flat.append(jnp.concatenate(
                    [re * u_cos - im * u_sin, re * u_sin + im * u_cos], 0
                ).astype(BF16))
            out = dot(g_last, jnp.concatenate(flat, 1))
            for c in range(group):
                for m, ref in enumerate((conv_wide, back_wide, tapg_wide)):
                    at = (3 * c + m) * LANES
                    ref[pick(c), :] = out[:, at:at + LANES]
            return carry

        lax.fori_loop(0, part // group, some_channels, jnp.int32(0))

        biases = jnp.broadcast_to(bias[chan_lo:chan_lo + part, :], (part, LANES))
        for d in range(n_ctx):
            for j in range(tiles):
                at = (d * tiles + j) * part
                cols = slice(j * LANES, (j + 1) * LANES)
                out_send[h, d, 0, :, cols] = (
                    back_wide[at:at + part, :] + biases * sig_wide[at:at + part, :]
                ).astype(BF16)
                out_send[h, d, 1, :, cols] = (
                    conv_wide[at:at + part, :] + biases * val_wide[at:at + part, :]
                ).astype(BF16)
        for peer in ctx_peers:
            to_ctx(
                out_send.at[h, peer], out_recv.at[h, ctx],
                out_ss.at[h, peer], out_rs.at[h, ctx], peer,
            ).start()
        out_recv[h, ctx] = out_send[h, ctx]
        span = lag_tiles * part
        for e in range(n_ex):
            block = tapg_wide[e * span:(e + 1) * span, :]
            square = square + jnp.sum((block * block).reshape(span // 8, 8, LANES), 0)
            grad_send[h, e] = block.astype(BF16)
        for peer in ex_peers:
            to_ex(
                grad_send.at[h, peer], grad_recv.at[h, ex],
                grad_ss.at[h, peer], grad_rs.at[h, ex], peer,
            ).start()
        grad_recv[h, ex] = grad_send[h, ex]

    sq_send[...] = square
    for peer in ctx_peers:
        to_ctx(sq_send, sq_recv.at[ctx], sq_ss.at[peer], sq_rs.at[ctx], peer).start()
    sq_recv[ctx] = square
    for peer in ctx_peers:
        to_ctx(sq_send, sq_recv.at[peer], sq_ss.at[peer], sq_rs.at[peer], peer).wait_recv()
    total = jnp.sum(jnp.sum(sq_recv[...], 0), keepdims=True)
    rms = jnp.sqrt(total / float(rows * LANES * depth) + EPS)
    limit = bound[...].astype(F32)
    factor = jnp.broadcast_to(jnp.minimum(1.0, limit / rms), (8, LANES))
    fac_send[...] = factor
    for peer in ex_peers:
        to_ex(fac_send, fac_recv.at[ex], fac_ss.at[peer], fac_rs.at[ex], peer).start()
    fac_recv[ex] = factor
    for peer in ex_peers:
        to_ex(fac_send, fac_recv.at[peer], fac_ss.at[peer], fac_rs.at[peer], peer).wait_recv()
    for h in range(halves):
        for peer in ex_peers:
            to_ex(
                grad_send.at[h, peer], grad_recv.at[h, peer],
                grad_ss.at[h, peer], grad_rs.at[h, peer], peer,
            ).wait_recv()
        for j in range(lag_tiles):
            acc = jnp.zeros((part, LANES), F32)
            for e in range(n_ex):
                acc = acc + fac_recv[e, 0:1, :] * grad_recv[h, e, j * part:(j + 1) * part, :].astype(F32)
            filter_grad[h * part:(h + 1) * part, j * LANES:(j + 1) * LANES] = acc

    for h in range(halves):
        for peer in ctx_peers:
            to_ctx(
                out_send.at[h, peer], out_recv.at[h, peer],
                out_ss.at[h, peer], out_rs.at[h, peer], peer,
            ).wait_recv()
    turned = (((0,), (0,)), ((), ()))
    order = [(d, h) for d in range(n_ctx) for h in range(halves)]
    for lo in range(0, tokens, width):
        cols = slice(lo, lo + width)
        value_grad = stack_rows([out_recv[h, d, 0, :, cols] for d, h in order])
        state = stack_rows([out_recv[h, d, 1, :, cols] for d, h in order])
        cot = jnp.where(keep[:, cols], cotangent[0, :, cols].astype(F32), 0.0)
        gate_grad = (state.astype(F32) * cot).astype(BF16)
        result = lax.dot_general(w_value[...], value_grad, turned, preferred_element_type=F32)
        result = result + lax.dot_general(w_gate[...], gate_grad, turned, preferred_element_type=F32)
        input_grad[0, :, cols] = result.astype(BF16)

    for peer in ex_peers:
        to_ex(tap_send, tap_recv.at[ex], tap_ss.at[peer], tap_rs.at[ex], peer).wait_send()
        to_ex(fac_send, fac_recv.at[ex], fac_ss.at[peer], fac_rs.at[ex], peer).wait_send()
        for h in range(halves):
            to_ex(
                grad_send.at[h, peer], grad_recv.at[h, ex],
                grad_ss.at[h, peer], grad_rs.at[h, ex], peer,
            ).wait_send()
    for peer in ctx_peers:
        to_ctx(sq_send, sq_recv.at[ctx], sq_ss.at[peer], sq_rs.at[ctx], peer).wait_send()
        for h in range(halves):
            to_ctx(
                in_send.at[h, peer], in_recv.at[h, ctx],
                in_ss.at[h, peer], in_rs.at[h, ctx], peer,
            ).wait_send()
            to_ctx(
                out_send.at[h, peer], out_recv.at[h, ctx],
                out_ss.at[h, peer], out_rs.at[h, ctx], peer,
            ).wait_send()


def on_device(n_ctx, n_ex, stream, cotangent, ids, bound, w_value, w_gate, taps, bias):
    tokens = stream.shape[2]
    chans, lags = taps.shape
    halves = 2 if chans % 32 == 0 else 1
    part = chans // halves
    group = min(4, part)
    rows = n_ctx * tokens // LANES
    span = lags // LANES * part
    vmem = pl.BlockSpec(memory_space=pltpu.VMEM)
    dma = pltpu.SemaphoreType.DMA
    wide = pltpu.VMEM((rows * part, LANES), F32)
    across = pltpu.VMEM((halves, n_ctx, 2, part, tokens), BF16)
    return pl.pallas_call(
        functools.partial(kernel, n_ctx, n_ex, halves, group),
        out_shape=(
            jax.ShapeDtypeStruct(stream.shape, BF16),
            jax.ShapeDtypeStruct(taps.shape, F32),
        ),
        in_specs=[vmem] * 13,
        out_specs=(vmem, vmem),
        scratch_shapes=[
            across, across, across, across,
            pltpu.VMEM((chans, lags), BF16),
            pltpu.VMEM((n_ex, chans, lags), BF16),
            pltpu.VMEM((halves, n_ex, span, LANES), BF16),
            pltpu.VMEM((halves, n_ex, span, LANES), BF16),
            pltpu.VMEM((8, LANES), F32),
            pltpu.VMEM((n_ctx, 8, LANES), F32),
            pltpu.VMEM((8, LANES), F32),
            pltpu.VMEM((n_ex, 8, LANES), F32),
            wide, wide, wide, wide, wide, wide,
            dma((halves, n_ctx)), dma((halves, n_ctx)),
            dma((halves, n_ctx)), dma((halves, n_ctx)),
            dma((n_ex,)), dma((n_ex,)),
            dma((halves, n_ex)), dma((halves, n_ex)),
            dma((n_ctx,)), dma((n_ctx,)),
            dma((n_ex,)), dma((n_ex,)),
        ],
        compiler_params=pltpu.CompilerParams(collective_id=0, has_side_effects=True),
    )(
        stream, cotangent, ids, bound.reshape(1, 1), w_value, w_gate, taps, bias[:, None],
        *tables(rows),
    )


def solution(mesh):
    in_specs = (
        P("ex", None, "ctx"),
        P("ex", None, "ctx"),
        P("ex", "ctx"),
        P("ex"),
        P(),
        P(),
        P("ctx", "ex"),
        P("ctx"),
    )
    out_specs = (P("ex", None, "ctx"), P("ctx", "ex"))
    return jax.shard_map(
        functools.partial(on_device, mesh.shape["ctx"], mesh.shape["ex"]),
        mesh=mesh, in_specs=in_specs, out_specs=out_specs, check_vma=False,
    )
```

```python
import functools
import math

import jax
import jax.numpy as jnp
import numpy as np
from jax import lax
from jax.experimental import pallas as pl
from jax.experimental.pallas import tpu as pltpu
from jax.sharding import PartitionSpec as P

LANES = 128
UNKNOWN = 4
EPS = 1e-06
VMEM_ALL = 67043328
F32 = jnp.float32
BF16 = jnp.bfloat16
MESH = pl.DeviceIdType.MESH


def tables(rows):
    whole = 2 * rows * LANES
    ka = np.arange(rows) + 0.5
    a = np.arange(rows)
    r = np.arange(LANES)
    outer = 2 * math.pi * ka[:, None] * a[None, :] / (2 * rows)
    inner = 2 * math.pi * (r[:, None] * r[None, :] % LANES) / LANES
    twist = 2 * math.pi * ka[:, None] * r[None, :] / whole
    cos, sin = np.cos(inner), np.sin(inner)
    first = np.concatenate([np.cos(outer), -np.sin(outer)], 0)
    last = np.concatenate([np.cos(outer).T, -np.sin(outer).T], 1)
    second = np.block([[cos, -sin], [sin, cos]])
    third = np.block([[cos, sin], [-sin, cos]])
    twist = np.stack([np.cos(twist), np.sin(twist)])
    return (
        jnp.asarray(first, BF16),
        jnp.asarray(second, BF16),
        jnp.asarray(third, BF16),
        jnp.asarray(last, BF16),
        jnp.asarray(twist, F32),
    )


def dot(x, y):
    return jnp.dot(x, y, preferred_element_type=F32)


def partners(me, count):
    if count & (count - 1):
        return [lax.rem(me + i, count) for i in range(1, count)]
    out = []
    for i in sorted(range(1, count), key=lambda i: -bin(i >> 1).count("1")):
        peer, bit = me, 1
        while bit < count:
            if i & bit:
                peer = peer + bit - 2 * bit * lax.rem(lax.div(me, bit), 2)
            bit *= 2
        out.append(peer)
    return out


def kernel(
    n_ctx, n_ex, halves, group,
    bound, *refs,
):
    sources, refs = refs[:12], refs[12:]
    (value_grad, gate_grad, filter_sum, w_value, w_gate), refs = refs[:5], refs[5:]
    (stream, cotangent, ids, taps, bias, first, second, third, last, twist), refs = refs[:10], refs[10:]
    (
    in_send, in_recv, out_send, out_recv, tap_send, tap_recv, grad_send, grad_recv,
    sq_send, sq_recv, fac_send, fac_recv,
    val_wide, sig_wide, fil_wide, conv_wide, back_wide, tapg_wide,
    in_ss, in_rs, out_ss, out_rs, tap_ss, tap_rs, grad_ss, grad_rs,
    sq_ss, sq_rs, fac_ss, fac_rs, load_sem,
    ) = refs
    held = (stream, w_value, w_gate, ids, cotangent, taps, bias, first, second, third, last, twist)
    loads = [
        pltpu.make_async_copy(src, dst, load_sem.at[i])
        for i, (src, dst) in enumerate(zip(sources, held))
    ]
    for load in loads:
        load.start()
    ex = lax.axis_index("ex")
    ctx = lax.axis_index("ctx")
    ctx_peers = partners(ctx, n_ctx)
    ex_peers = [lax.rem(ex + i, n_ex) for i in range(1, n_ex)]
    depth = stream.shape[1]
    tokens = stream.shape[2]
    chans = taps.shape[0]
    part = chans // halves
    tiles = tokens // LANES
    rows = n_ctx * tiles
    lag_tiles = rows // n_ex

    def to_ctx(src, dst, ss, rs, peer):
        return pltpu.make_async_remote_copy(
            src_ref=src, dst_ref=dst, send_sem=ss, recv_sem=rs,
            device_id=(ex, peer), device_id_type=MESH,
        )

    def to_ex(src, dst, ss, rs, peer):
        return pltpu.make_async_remote_copy(
            src_ref=src, dst_ref=dst, send_sem=ss, recv_sem=rs,
            device_id=(peer, ctx), device_id_type=MESH,
        )

    barrier = pltpu.get_barrier_semaphore()
    for peer in ctx_peers:
        pl.semaphore_signal(barrier, inc=1, device_id=(ex, peer), device_id_type=MESH)
    for peer in ex_peers:
        pl.semaphore_signal(barrier, inc=1, device_id=(peer, ctx), device_id_type=MESH)

    for load in loads[:6]:
        load.wait()
    for h in range(halves):
        tap_send[h] = taps[h * part:(h + 1) * part, :].astype(BF16)
    keep = ids[...] != UNKNOWN

    width = min(256, tokens)
    tok = stream[0]
    for lo in range(0, tokens, width):
        cols = slice(lo, lo + width)
        value = dot(w_value[...], tok[:, cols])
        gate = dot(w_gate[...], tok[:, cols]).astype(BF16).astype(F32)
        cot = jnp.where(keep[:, cols], cotangent[0, :, cols].astype(F32), 0.0)
        signal = gate * cot
        for d in range(n_ctx):
            for h in range(halves):
                at = d * chans + h * part
                in_send[h, d, 0, :, cols] = value[at:at + part].astype(BF16)
                in_send[h, d, 1, :, cols] = signal[at:at + part].astype(BF16)

    pl.semaphore_wait(barrier, n_ctx - 1 + n_ex - 1)
    for h in range(halves):
        for peer in ex_peers:
            to_ex(
                tap_send.at[h], tap_recv.at[h, ex],
                tap_ss.at[h, peer], tap_rs.at[h, ex], peer,
            ).start()
        for peer in ctx_peers:
            to_ctx(
                in_send.at[h, peer], in_recv.at[h, ctx],
                in_ss.at[h, peer], in_rs.at[h, ctx], peer,
            ).start()
    for h in range(halves):
        tap_recv[h, ex] = tap_send[h]
        in_recv[h, ctx] = in_send[h, ctx]
    for load in loads[6:]:
        load.wait()
    eye = lax.broadcasted_iota(jnp.int32, (chans, chans), 0) == lax.broadcasted_iota(
        jnp.int32, (chans, chans), 1
    )
    bias_col = jnp.sum(jnp.where(eye, bias[...], 0.0), 1, keepdims=True)

    g_first, g_second, g_third, g_last = first[...], second[...], third[...], last[...]
    scale = 1.0 / (rows * LANES)
    square = jnp.zeros((8, LANES), F32)

    for h in range(halves):
        chan_lo = h * part
        for peer in ctx_peers:
            to_ctx(
                in_send.at[h, peer], in_recv.at[h, peer],
                in_ss.at[h, peer], in_rs.at[h, peer], peer,
            ).wait_recv()
        for peer in ex_peers:
            to_ex(
                tap_send.at[h], tap_recv.at[h, peer],
                tap_ss.at[h, peer], tap_rs.at[h, peer], peer,
            ).wait_recv()
        for e in range(n_ex):
            for j in range(lag_tiles):
                at = (e * lag_tiles + j) * part
                fil_wide[at:at + part, :] = tap_recv[h, e, :, j * LANES:(j + 1) * LANES].astype(F32)
        for d in range(n_ctx):
            for j in range(tiles):
                at = (d * tiles + j) * part
                cols = slice(j * LANES, (j + 1) * LANES)
                val_wide[at:at + part, :] = in_recv[h, d, 0, :, cols].astype(F32)
                sig_wide[at:at + part, :] = in_recv[h, d, 1, :, cols].astype(F32)

        def some_channels(step, carry):
            base = step * group
            pick = lambda c: pl.ds(base + c, rows, stride=part)
            flat = []
            for c in range(group):
                for ref in (fil_wide, val_wide, sig_wide):
                    flat.append(ref[pick(c), :].astype(BF16))
            mid = dot(g_first, jnp.concatenate(flat, 1))
            t_cos, t_sin = twist[0], twist[1]
            blocks = []
            for m in range(3 * group):
                re = mid[:rows, m * LANES:(m + 1) * LANES]
                im = mid[rows:, m * LANES:(m + 1) * LANES]
                blocks.append(jnp.concatenate(
                    [re * t_cos + im * t_sin, im * t_cos - re * t_sin], 1
                ).astype(BF16))
            spec = dot(jnp.concatenate(blocks, 0), g_second)
            blocks = []
            for c in range(group):
                parts = []
                for m in range(3):
                    at = (3 * c + m) * rows
                    parts.append(spec[at:at + rows, :LANES])
                    parts.append(spec[at:at + rows, LANES:])
                fr, fi, vr, vi, sr, si = parts
                blocks.append(jnp.concatenate([fr * vr - fi * vi, fr * vi + fi * vr], 1).astype(BF16))
                blocks.append(jnp.concatenate([fr * sr + fi * si, fr * si - fi * sr], 1).astype(BF16))
                blocks.append(jnp.concatenate([sr * vr + si * vi, si * vr - sr * vi], 1).astype(BF16))
            back = dot(jnp.concatenate(blocks, 0), g_third)
            flat = []
            u_cos, u_sin = t_cos * scale, t_sin * scale
            for m in range(3 * group):
                re = back[m * rows:(m + 1) * rows, :LANES]
                im = back[m * rows:(m + 1) * rows, LANES:]
                flat.append(jnp.concatenate(
                    [re * u_cos - im * u_sin, re * u_sin + im * u_cos], 0
                ).astype(BF16))
            out = dot(g_last, jnp.concatenate(flat, 1))
            for c in range(group):
                for m, ref in enumerate((conv_wide, back_wide, tapg_wide)):
                    at = (3 * c + m) * LANES
                    ref[pick(c), :] = out[:, at:at + LANES]
            return carry

        lax.fori_loop(0, part // group, some_channels, jnp.int32(0))

        biases = jnp.broadcast_to(bias_col[chan_lo:chan_lo + part, :], (part, LANES))

        def results(d):
            for j in range(tiles):
                at = pl.ds(pl.multiple_of((d * tiles + j) * part, part), part)
                cols = slice(j * LANES, (j + 1) * LANES)
                out_send[h, d, 0, :, cols] = (
                    back_wide[at, :] + biases * sig_wide[at, :]
                ).astype(BF16)
                out_send[h, d, 1, :, cols] = (
                    conv_wide[at, :] + biases * val_wide[at, :]
                ).astype(BF16)

        def lags_out(square):
            span = lag_tiles * part
            for e in range(n_ex):
                block = tapg_wide[e * span:(e + 1) * span, :]
                square = square + jnp.sum((block * block).reshape(span // 8, 8, LANES), 0)
                grad_send[h, e] = block.astype(BF16)
            for peer in ex_peers:
                to_ex(
                    grad_send.at[h, peer], grad_recv.at[h, ex],
                    grad_ss.at[h, peer], grad_rs.at[h, ex], peer,
                ).start()
            grad_recv[h, ex] = grad_send[h, ex]
            return square

        if h == halves - 1:
            square = lags_out(square)
            sq_send[...] = square
            for peer in ctx_peers:
                to_ctx(sq_send, sq_recv.at[ctx], sq_ss.at[peer], sq_rs.at[ctx], peer).start()
            sq_recv[ctx] = square
        for peer in ctx_peers:
            results(peer)
            to_ctx(
                out_send.at[h, peer], out_recv.at[h, ctx],
                out_ss.at[h, peer], out_rs.at[h, ctx], peer,
            ).start()
        results(ctx)
        out_recv[h, ctx] = out_send[h, ctx]
        if h < halves - 1:
            square = lags_out(square)

    def tokens_back(h):
        for peer in ctx_peers:
            to_ctx(
                out_send.at[h, peer], out_recv.at[h, peer],
                out_ss.at[h, peer], out_rs.at[h, peer], peer,
            ).wait_recv()
        for d in range(n_ctx):
            at = d * chans + h * part
            cot = jnp.where(keep, cotangent[0, at:at + part, :].astype(F32), 0.0)
            value_grad[at:at + part, :] = out_recv[h, d, 0]
            gate_grad[at:at + part, :] = (out_recv[h, d, 1].astype(F32) * cot).astype(BF16)

    for h in range(halves - 1):
        tokens_back(h)
    for peer in ctx_peers:
        to_ctx(sq_send, sq_recv.at[peer], sq_ss.at[peer], sq_rs.at[peer], peer).wait_recv()
    total = jnp.sum(jnp.sum(sq_recv[...], 0), keepdims=True)
    rms = jnp.sqrt(total / float(rows * LANES * depth) + EPS)
    limit = bound[0].astype(F32)
    factor = jnp.broadcast_to(jnp.minimum(1.0, limit / rms), (8, LANES))
    fac_send[...] = factor
    for peer in ex_peers:
        to_ex(fac_send, fac_recv.at[ex], fac_ss.at[peer], fac_rs.at[ex], peer).start()
    fac_recv[ex] = factor
    for peer in ex_peers:
        to_ex(fac_send, fac_recv.at[peer], fac_ss.at[peer], fac_rs.at[peer], peer).wait_recv()
    for h in range(halves):
        for peer in ex_peers:
            to_ex(
                grad_send.at[h, peer], grad_recv.at[h, peer],
                grad_ss.at[h, peer], grad_rs.at[h, peer], peer,
            ).wait_recv()
        for j in range(lag_tiles):
            acc = jnp.zeros((part, LANES), F32)
            for e in range(n_ex):
                acc = acc + fac_recv[e, 0:1, :] * grad_recv[h, e, j * part:(j + 1) * part, :].astype(F32)
            filter_sum[h * part:(h + 1) * part, j * LANES:(j + 1) * LANES] = acc

    tokens_back(halves - 1)

    for peer in ex_peers:
        to_ex(fac_send, fac_recv.at[ex], fac_ss.at[peer], fac_rs.at[ex], peer).wait_send()
        for h in range(halves):
            to_ex(
                tap_send.at[h], tap_recv.at[h, ex],
                tap_ss.at[h, peer], tap_rs.at[h, ex], peer,
            ).wait_send()
            to_ex(
                grad_send.at[h, peer], grad_recv.at[h, ex],
                grad_ss.at[h, peer], grad_rs.at[h, ex], peer,
            ).wait_send()
    for peer in ctx_peers:
        to_ctx(sq_send, sq_recv.at[ctx], sq_ss.at[peer], sq_rs.at[ctx], peer).wait_send()
        for h in range(halves):
            to_ctx(
                in_send.at[h, peer], in_recv.at[h, ctx],
                in_ss.at[h, peer], in_rs.at[h, ctx], peer,
            ).wait_send()
            to_ctx(
                out_send.at[h, peer], out_recv.at[h, ctx],
                out_ss.at[h, peer], out_rs.at[h, ctx], peer,
            ).wait_send()


def finish(value_grad, gate_grad, w_value, w_gate, filter_sum, input_grad, filter_grad):
    turned = (((0,), (0,)), ((), ()))
    filter_grad[...] = filter_sum[...]
    tokens = value_grad.shape[1]
    width = min(256, tokens)
    for lo in range(0, tokens, width):
        cols = slice(lo, lo + width)
        result = lax.dot_general(w_value[...], value_grad[:, cols], turned, preferred_element_type=F32)
        result = result + lax.dot_general(w_gate[...], gate_grad[:, cols], turned, preferred_element_type=F32)
        input_grad[0, :, cols] = result.astype(BF16)


def on_device(n_ctx, n_ex, stream, cotangent, ids, bound, w_value, w_gate, taps, bias):
    tokens = stream.shape[2]
    chans, lags = taps.shape
    halves = 2 if chans % 32 == 0 else 1
    part = chans // halves
    group = min(4, part)
    rows = n_ctx * tokens // LANES
    span = lags // LANES * part
    vmem = pl.BlockSpec(memory_space=pltpu.VMEM)
    dma = pltpu.SemaphoreType.DMA
    wide = pltpu.VMEM((rows * part, LANES), F32)
    across = pltpu.VMEM((halves, n_ctx, 2, part, tokens), BF16)
    depth = stream.shape[1]
    operands = (
        stream, w_value, w_gate, ids, cotangent, taps, bias.reshape(1, -1), *tables(rows),
    )
    loaded = [pltpu.VMEM(operands[i].shape, operands[i].dtype) for i in (0, 4, 3, 5, 6, 7, 8, 9, 10, 11)]
    value_grad, gate_grad, filter_sum, w_value, w_gate = pl.pallas_call(
        functools.partial(kernel, n_ctx, n_ex, halves, group),
        out_shape=(
            jax.ShapeDtypeStruct((depth, tokens), BF16),
            jax.ShapeDtypeStruct((depth, tokens), BF16),
            jax.ShapeDtypeStruct(taps.shape, F32),
            jax.ShapeDtypeStruct(w_value.shape, w_value.dtype),
            jax.ShapeDtypeStruct(w_gate.shape, w_gate.dtype),
        ),
        in_specs=[pl.BlockSpec(memory_space=pltpu.SMEM)] + [pl.BlockSpec(memory_space=pltpu.HBM)] * 12,
        out_specs=(vmem,) * 5,
        scratch_shapes=loaded + [
            across, across, across, across,
            pltpu.VMEM((halves, part, lags), BF16),
            pltpu.VMEM((halves, n_ex, part, lags), BF16),
            pltpu.VMEM((halves, n_ex, span, LANES), BF16),
            pltpu.VMEM((halves, n_ex, span, LANES), BF16),
            pltpu.VMEM((8, LANES), F32),
            pltpu.VMEM((n_ctx, 8, LANES), F32),
            pltpu.VMEM((8, LANES), F32),
            pltpu.VMEM((n_ex, 8, LANES), F32),
            wide, wide, wide, wide, wide, wide,
            dma((halves, n_ctx)), dma((halves, n_ctx)),
            dma((halves, n_ctx)), dma((halves, n_ctx)),
            dma((halves, n_ex)), dma((halves, n_ex)),
            dma((halves, n_ex)), dma((halves, n_ex)),
            dma((n_ctx,)), dma((n_ctx,)),
            dma((n_ex,)), dma((n_ex,)),
            dma((12,)),
        ],
        compiler_params=pltpu.CompilerParams(collective_id=0, has_side_effects=True, vmem_limit_bytes=VMEM_ALL),
    )(bound, *operands)
    return pl.pallas_call(
        finish,
        out_shape=(
            jax.ShapeDtypeStruct(stream.shape, BF16),
            jax.ShapeDtypeStruct(taps.shape, F32),
        ),
        in_specs=[vmem] * 5,
        out_specs=(vmem, vmem),
        compiler_params=pltpu.CompilerParams(vmem_limit_bytes=VMEM_ALL),
    )(value_grad, gate_grad, w_value, w_gate, filter_sum)


def solution(mesh):
    in_specs = (
        P("ex", None, "ctx"),
        P("ex", None, "ctx"),
        P("ex", "ctx"),
        P("ex"),
        P(),
        P(),
        P("ctx", "ex"),
        P("ctx"),
    )
    out_specs = (P("ex", None, "ctx"), P("ctx", "ex"))
    return jax.shard_map(
        functools.partial(on_device, mesh.shape["ctx"], mesh.shape["ex"]),
        mesh=mesh, in_specs=in_specs, out_specs=out_specs, check_vma=False,
    )
```

```python
import functools
import math

import jax
import jax.numpy as jnp
import numpy as np
from jax import lax
from jax.experimental import pallas as pl
from jax.experimental.pallas import tpu as pltpu
from jax.sharding import PartitionSpec as P

LANES = 128
UNKNOWN = 4
EPS = 1e-06
VMEM_ALL = 67043328
F32 = jnp.float32
BF16 = jnp.bfloat16
MESH = pl.DeviceIdType.MESH


def tables(rows):
    whole = 2 * rows * LANES
    ka = np.arange(rows) + 0.5
    a = np.arange(rows)
    r = np.arange(LANES)
    outer = 2 * math.pi * ka[:, None] * a[None, :] / (2 * rows)
    inner = 2 * math.pi * (r[:, None] * r[None, :] % LANES) / LANES
    twist = 2 * math.pi * ka[:, None] * r[None, :] / whole
    cos, sin = np.cos(inner), np.sin(inner)
    first = np.concatenate([np.cos(outer), -np.sin(outer)], 0)
    last = np.concatenate([np.cos(outer).T, -np.sin(outer).T], 1)
    second = np.block([[cos, -sin], [sin, cos]])
    third = np.block([[cos, sin], [-sin, cos]])
    twist = np.stack([np.cos(twist), np.sin(twist)])
    return (
        jnp.asarray(first, BF16),
        jnp.asarray(second, BF16),
        jnp.asarray(third, BF16),
        jnp.asarray(last, BF16),
        jnp.asarray(twist, F32),
    )


def dot(x, y):
    return jnp.dot(x, y, preferred_element_type=F32)


def partners(me, count):
    if count & (count - 1):
        return [lax.rem(me + i, count) for i in range(1, count)]
    out = []
    for i in sorted(range(1, count), key=lambda i: -bin(i >> 1).count("1")):
        peer, bit = me, 1
        while bit < count:
            if i & bit:
                peer = peer + bit - 2 * bit * lax.rem(lax.div(me, bit), 2)
            bit *= 2
        out.append(peer)
    return out


def kernel(
    n_ctx, n_ex, halves, group,
    bound, *refs,
):
    sources, refs = refs[:12], refs[12:]
    (value_grad, gate_grad, filter_sum, w_value, w_gate), refs = refs[:5], refs[5:]
    (stream, cotangent, ids, taps, bias, first, second, third, last, twist), refs = refs[:10], refs[10:]
    (
    in_send, in_recv, out_send, out_recv, tap_send, tap_recv, grad_send, grad_recv,
    sq_send, sq_recv, fac_send, fac_recv,
    val_wide, sig_wide, fil_wide, conv_wide, back_wide, tapg_wide,
    in_ss, in_rs, out_ss, out_rs, tap_ss, tap_rs, grad_ss, grad_rs,
    sq_ss, sq_rs, fac_ss, fac_rs, load_sem,
    ) = refs
    held = (stream, w_value, w_gate, ids, cotangent, taps, bias, first, second, third, last, twist)
    loads = [
        pltpu.make_async_copy(src, dst, load_sem.at[i])
        for i, (src, dst) in enumerate(zip(sources, held))
    ]
    for load in loads:
        load.start()
    ex = lax.axis_index("ex")
    ctx = lax.axis_index("ctx")
    ctx_peers = partners(ctx, n_ctx)
    ex_peers = [lax.rem(ex + i, n_ex) for i in range(1, n_ex)]
    depth = stream.shape[1]
    tokens = stream.shape[2]
    chans = taps.shape[0]
    part = chans // halves
    tiles = tokens // LANES
    rows = n_ctx * tiles
    lag_tiles = rows // n_ex

    def to_ctx(src, dst, ss, rs, peer):
        return pltpu.make_async_remote_copy(
            src_ref=src, dst_ref=dst, send_sem=ss, recv_sem=rs,
            device_id=(ex, peer), device_id_type=MESH,
        )

    def to_ex(src, dst, ss, rs, peer):
        return pltpu.make_async_remote_copy(
            src_ref=src, dst_ref=dst, send_sem=ss, recv_sem=rs,
            device_id=(peer, ctx), device_id_type=MESH,
        )

    barrier = pltpu.get_barrier_semaphore()
    for peer in ctx_peers:
        pl.semaphore_signal(barrier, inc=1, device_id=(ex, peer), device_id_type=MESH)
    for peer in ex_peers:
        pl.semaphore_signal(barrier, inc=1, device_id=(peer, ctx), device_id_type=MESH)

    for load in loads[:6]:
        load.wait()
    for h in range(halves):
        tap_send[h] = taps[h * part:(h + 1) * part, :].astype(BF16)
    keep = ids[...] != UNKNOWN

    width = min(256, tokens)
    tok = stream[0]
    for lo in range(0, tokens, width):
        cols = slice(lo, lo + width)
        value = dot(w_value[...], tok[:, cols])
        gate = dot(w_gate[...], tok[:, cols]).astype(BF16).astype(F32)
        cot = jnp.where(keep[:, cols], cotangent[0, :, cols].astype(F32), 0.0)
        signal = gate * cot
        for d in range(n_ctx):
            for h in range(halves):
                at = d * chans + h * part
                in_send[h, d, 0, :, cols] = value[at:at + part].astype(BF16)
                in_send[h, d, 1, :, cols] = signal[at:at + part].astype(BF16)

    pl.semaphore_wait(barrier, n_ctx - 1 + n_ex - 1)
    for h in range(halves):
        for peer in ex_peers:
            to_ex(
                tap_send.at[h], tap_recv.at[h, ex],
                tap_ss.at[h, peer], tap_rs.at[h, ex], peer,
            ).start()
        for peer in ctx_peers:
            to_ctx(
                in_send.at[h, peer], in_recv.at[h, ctx],
                in_ss.at[h, peer], in_rs.at[h, ctx], peer,
            ).start()
    for h in range(halves):
        tap_recv[h, ex] = tap_send[h]
        in_recv[h, ctx] = in_send[h, ctx]
    for load in loads[6:]:
        load.wait()
    eye = lax.broadcasted_iota(jnp.int32, (chans, chans), 0) == lax.broadcasted_iota(
        jnp.int32, (chans, chans), 1
    )
    bias_col = jnp.sum(jnp.where(eye, bias[...], 0.0), 1, keepdims=True)

    g_first, g_second, g_third, g_last = first[...], second[...], third[...], last[...]
    scale = 1.0 / (rows * LANES)
    square = jnp.zeros((8, LANES), F32)

    for h in range(halves):
        chan_lo = h * part
        for peer in ctx_peers:
            to_ctx(
                in_send.at[h, peer], in_recv.at[h, peer],
                in_ss.at[h, peer], in_rs.at[h, peer], peer,
            ).wait_recv()
        for peer in ex_peers:
            to_ex(
                tap_send.at[h], tap_recv.at[h, peer],
                tap_ss.at[h, peer], tap_rs.at[h, peer], peer,
            ).wait_recv()
        for e in range(n_ex):
            for j in range(lag_tiles):
                at = (e * lag_tiles + j) * part
                fil_wide[at:at + part, :] = tap_recv[h, e, :, j * LANES:(j + 1) * LANES].astype(F32)
        for d in range(n_ctx):
            for j in range(tiles):
                at = (d * tiles + j) * part
                cols = slice(j * LANES, (j + 1) * LANES)
                val_wide[at:at + part, :] = in_recv[h, d, 0, :, cols].astype(F32)
                sig_wide[at:at + part, :] = in_recv[h, d, 1, :, cols].astype(F32)

        def some_channels(step, carry):
            base = step * group
            pick = lambda c: pl.ds(base + c, rows, stride=part)
            flat = []
            for c in range(group):
                for ref in (fil_wide, val_wide, sig_wide):
                    flat.append(ref[pick(c), :].astype(BF16))
            mid = dot(g_first, jnp.concatenate(flat, 1))
            t_cos, t_sin = twist[0], twist[1]
            blocks = []
            for m in range(3 * group):
                re = mid[:rows, m * LANES:(m + 1) * LANES]
                im = mid[rows:, m * LANES:(m + 1) * LANES]
                blocks.append(jnp.concatenate(
                    [re * t_cos + im * t_sin, im * t_cos - re * t_sin], 1
                ).astype(BF16))
            spec = dot(jnp.concatenate(blocks, 0), g_second)
            blocks = []
            for c in range(group):
                parts = []
                for m in range(3):
                    at = (3 * c + m) * rows
                    parts.append(spec[at:at + rows, :LANES])
                    parts.append(spec[at:at + rows, LANES:])
                fr, fi, vr, vi, sr, si = parts
                blocks.append(jnp.concatenate([fr * vr - fi * vi, fr * vi + fi * vr], 1).astype(BF16))
                blocks.append(jnp.concatenate([fr * sr + fi * si, fr * si - fi * sr], 1).astype(BF16))
                blocks.append(jnp.concatenate([sr * vr + si * vi, si * vr - sr * vi], 1).astype(BF16))
            back = dot(jnp.concatenate(blocks, 0), g_third)
            flat = []
            u_cos, u_sin = t_cos * scale, t_sin * scale
            for m in range(3 * group):
                re = back[m * rows:(m + 1) * rows, :LANES]
                im = back[m * rows:(m + 1) * rows, LANES:]
                flat.append(jnp.concatenate(
                    [re * u_cos - im * u_sin, re * u_sin + im * u_cos], 0
                ).astype(BF16))
            out = dot(g_last, jnp.concatenate(flat, 1))
            for c in range(group):
                for m, ref in enumerate((conv_wide, back_wide, tapg_wide)):
                    at = (3 * c + m) * LANES
                    ref[pick(c), :] = out[:, at:at + LANES]
            return carry

        lax.fori_loop(0, part // group, some_channels, jnp.int32(0))

        biases = jnp.broadcast_to(bias_col[chan_lo:chan_lo + part, :], (part, LANES))

        def results(d):
            for j in range(tiles):
                at = pl.ds(pl.multiple_of((d * tiles + j) * part, part), part)
                cols = slice(j * LANES, (j + 1) * LANES)
                out_send[h, d, 0, :, cols] = (
                    back_wide[at, :] + biases * sig_wide[at, :]
                ).astype(BF16)
                out_send[h, d, 1, :, cols] = (
                    conv_wide[at, :] + biases * val_wide[at, :]
                ).astype(BF16)

        def lags_out(square):
            span = lag_tiles * part
            for e in range(n_ex):
                block = tapg_wide[e * span:(e + 1) * span, :]
                square = square + jnp.sum((block * block).reshape(span // 8, 8, LANES), 0)
                grad_send[h, e] = block.astype(BF16)
            for peer in ex_peers:
                to_ex(
                    grad_send.at[h, peer], grad_recv.at[h, ex],
                    grad_ss.at[h, peer], grad_rs.at[h, ex], peer,
                ).start()
            grad_recv[h, ex] = grad_send[h, ex]
            return square

        if h == halves - 1:
            square = lags_out(square)
            sq_send[...] = square
            for peer in ctx_peers:
                to_ctx(sq_send, sq_recv.at[ctx], sq_ss.at[peer], sq_rs.at[ctx], peer).start()
            sq_recv[ctx] = square
        for peer in ctx_peers:
            results(peer)
            to_ctx(
                out_send.at[h, peer], out_recv.at[h, ctx],
                out_ss.at[h, peer], out_rs.at[h, ctx], peer,
            ).start()
        results(ctx)
        out_recv[h, ctx] = out_send[h, ctx]
        if h < halves - 1:
            square = lags_out(square)

    def tokens_back(h):
        for peer in ctx_peers:
            to_ctx(
                out_send.at[h, peer], out_recv.at[h, peer],
                out_ss.at[h, peer], out_rs.at[h, peer], peer,
            ).wait_recv()
        for d in range(n_ctx):
            at = d * chans + h * part
            cot = jnp.where(keep, cotangent[0, at:at + part, :].astype(F32), 0.0)
            value_grad[at:at + part, :] = out_recv[h, d, 0]
            gate_grad[at:at + part, :] = (out_recv[h, d, 1].astype(F32) * cot).astype(BF16)

    for h in range(halves - 1):
        tokens_back(h)
    for peer in ctx_peers:
        to_ctx(sq_send, sq_recv.at[peer], sq_ss.at[peer], sq_rs.at[peer], peer).wait_recv()
    total = jnp.sum(jnp.sum(sq_recv[...], 0), keepdims=True)
    rms = jnp.sqrt(total / float(rows * LANES * depth) + EPS)
    limit = bound[0].astype(F32)
    factor = jnp.broadcast_to(jnp.minimum(1.0, limit / rms), (8, LANES))
    fac_send[...] = factor
    for peer in ex_peers:
        to_ex(fac_send, fac_recv.at[ex], fac_ss.at[peer], fac_rs.at[ex], peer).start()
    fac_recv[ex] = factor
    for peer in ex_peers:
        to_ex(fac_send, fac_recv.at[peer], fac_ss.at[peer], fac_rs.at[peer], peer).wait_recv()
    for h in range(halves):
        for peer in ex_peers:
            to_ex(
                grad_send.at[h, peer], grad_recv.at[h, peer],
                grad_ss.at[h, peer], grad_rs.at[h, peer], peer,
            ).wait_recv()
        for j in range(lag_tiles):
            acc = jnp.zeros((part, LANES), F32)
            for e in range(n_ex):
                acc = acc + fac_recv[e, 0:1, :] * grad_recv[h, e, j * part:(j + 1) * part, :].astype(F32)
            filter_sum[h * part:(h + 1) * part, j * LANES:(j + 1) * LANES] = acc

    tokens_back(halves - 1)

    for peer in ex_peers:
        to_ex(fac_send, fac_recv.at[ex], fac_ss.at[peer], fac_rs.at[ex], peer).wait_send()
        for h in range(halves):
            to_ex(
                tap_send.at[h], tap_recv.at[h, ex],
                tap_ss.at[h, peer], tap_rs.at[h, ex], peer,
            ).wait_send()
            to_ex(
                grad_send.at[h, peer], grad_recv.at[h, ex],
                grad_ss.at[h, peer], grad_rs.at[h, ex], peer,
            ).wait_send()
    for peer in ctx_peers:
        to_ctx(sq_send, sq_recv.at[ctx], sq_ss.at[peer], sq_rs.at[ctx], peer).wait_send()
        for h in range(halves):
            to_ctx(
                in_send.at[h, peer], in_recv.at[h, ctx],
                in_ss.at[h, peer], in_rs.at[h, ctx], peer,
            ).wait_send()
            to_ctx(
                out_send.at[h, peer], out_recv.at[h, ctx],
                out_ss.at[h, peer], out_rs.at[h, ctx], peer,
            ).wait_send()


def finish(value_grad, gate_grad, w_value, w_gate, filter_sum, input_grad, filter_grad):
    turned = (((0,), (0,)), ((), ()))
    filter_grad[...] = filter_sum[...]
    tokens = value_grad.shape[1]
    width = min(256, tokens)
    for lo in range(0, tokens, width):
        cols = slice(lo, lo + width)
        result = lax.dot_general(w_value[...], value_grad[:, cols], turned, preferred_element_type=F32)
        result = result + lax.dot_general(w_gate[...], gate_grad[:, cols], turned, preferred_element_type=F32)
        input_grad[0, :, cols] = result.astype(BF16)


def on_device(n_ctx, n_ex, stream, cotangent, ids, bound, w_value, w_gate, taps, bias):
    tokens = stream.shape[2]
    chans, lags = taps.shape
    halves = 2 if chans % 32 == 0 else 1
    part = chans // halves
    group = min(8, part)
    rows = n_ctx * tokens // LANES
    span = lags // LANES * part
    vmem = pl.BlockSpec(memory_space=pltpu.VMEM)
    dma = pltpu.SemaphoreType.DMA
    wide = pltpu.VMEM((rows * part, LANES), F32)
    across = pltpu.VMEM((halves, n_ctx, 2, part, tokens), BF16)
    depth = stream.shape[1]
    operands = (
        stream, w_value, w_gate, ids, cotangent, taps, bias.reshape(1, -1), *tables(rows),
    )
    loaded = [pltpu.VMEM(operands[i].shape, operands[i].dtype) for i in (0, 4, 3, 5, 6, 7, 8, 9, 10, 11)]
    value_grad, gate_grad, filter_sum, w_value, w_gate = pl.pallas_call(
        functools.partial(kernel, n_ctx, n_ex, halves, group),
        out_shape=(
            jax.ShapeDtypeStruct((depth, tokens), BF16),
            jax.ShapeDtypeStruct((depth, tokens), BF16),
            jax.ShapeDtypeStruct(taps.shape, F32),
            jax.ShapeDtypeStruct(w_value.shape, w_value.dtype),
            jax.ShapeDtypeStruct(w_gate.shape, w_gate.dtype),
        ),
        in_specs=[pl.BlockSpec(memory_space=pltpu.SMEM)] + [pl.BlockSpec(memory_space=pltpu.HBM)] * 12,
        out_specs=(vmem,) * 5,
        scratch_shapes=loaded + [
            across, across, across, across,
            pltpu.VMEM((halves, part, lags), BF16),
            pltpu.VMEM((halves, n_ex, part, lags), BF16),
            pltpu.VMEM((halves, n_ex, span, LANES), BF16),
            pltpu.VMEM((halves, n_ex, span, LANES), BF16),
            pltpu.VMEM((8, LANES), F32),
            pltpu.VMEM((n_ctx, 8, LANES), F32),
            pltpu.VMEM((8, LANES), F32),
            pltpu.VMEM((n_ex, 8, LANES), F32),
            wide, wide, wide, wide, wide, wide,
            dma((halves, n_ctx)), dma((halves, n_ctx)),
            dma((halves, n_ctx)), dma((halves, n_ctx)),
            dma((halves, n_ex)), dma((halves, n_ex)),
            dma((halves, n_ex)), dma((halves, n_ex)),
            dma((n_ctx,)), dma((n_ctx,)),
            dma((n_ex,)), dma((n_ex,)),
            dma((12,)),
        ],
        compiler_params=pltpu.CompilerParams(collective_id=0, has_side_effects=True, vmem_limit_bytes=VMEM_ALL),
    )(bound, *operands)
    return pl.pallas_call(
        finish,
        out_shape=(
            jax.ShapeDtypeStruct(stream.shape, BF16),
            jax.ShapeDtypeStruct(taps.shape, F32),
        ),
        in_specs=[vmem] * 5,
        out_specs=(vmem, vmem),
        compiler_params=pltpu.CompilerParams(vmem_limit_bytes=VMEM_ALL),
    )(value_grad, gate_grad, w_value, w_gate, filter_sum)


def solution(mesh):
    in_specs = (
        P("ex", None, "ctx"),
        P("ex", None, "ctx"),
        P("ex", "ctx"),
        P("ex"),
        P(),
        P(),
        P("ctx", "ex"),
        P("ctx"),
    )
    out_specs = (P("ex", None, "ctx"), P("ctx", "ex"))
    return jax.shard_map(
        functools.partial(on_device, mesh.shape["ctx"], mesh.shape["ex"]),
        mesh=mesh, in_specs=in_specs, out_specs=out_specs, check_vma=False,
    )
```
